128 devices in a mesh: row: 16 (over z, y_lo, core), col: 8 (over y_hi, x).
Axes of the slice: x: 4, y: 4 (y_hi: 2, y_lo: 2; y = y_hi * 2 + y_lo), z: 4, core: 2. Of those that a mesh axis runs over, the one named last changes fastest.
Arguments:
- panels: bfloat16 [1024, 32, 256], P(('row', 'col')), may hold values from -21 to 21
- tiles: bfloat16 [6144, 256, 512], P(('row', 'col')), may hold values from -0.109375 to 0.109375
- tile_dst: int32 [6144], P(('row', 'col')), may hold values from 0 to 7
- tile_src: int32 [6144], P(('row', 'col')), may hold values from 0 to 127
- geometry: float32 [1024, 6, 256], P(('row', 'col')), may hold values from -5 to 5
- areas: float32 [1024, 256], P(('row', 'col')), may hold values from 0.25 to 2
- block_owner: int32 [1024, 1], P(('row', 'col')), may hold values from 0 to 7; in each aligned block of 8 rows (0 to 7, 8 to 15, ...) at most 2 rows name the same one
- block_slot: int32 [1024], P(('row', 'col')), may hold values from 0 to 3
Outputs:
- field: float32 [1024, 32, 256], P(('row', 'col'))
- shape_gradient: float32 [1024, 256], P(('row', 'col'))
The draws below stay inside these ranges and needn't reach their ends.
Inputs may be any that keep to these rules, and one draw needn't show every extreme that they name: Among the blocks of one device at most 2 have the same block_owner, and some device reaches 2.
All inputs are finite; a program needn't handle non-finite values.
Results may differ from the reference program's by a relative error of at most 0.0003.
Values may be sent and summed in bfloat16 or wider, within the bound.
A program may use at most 64 MiB of HBM per device.

```python
import math
import jax
import jax.numpy as jnp
import numpy as np
from jax import lax

BN = 256
NF = 16
CAP = 2
NBD = 8
TPD = 48
PD = 4
NB = 1024
NT = 6144
N_ROW = 16
N_COL = 8


def draw_panels(key, part):
    key_levels = jax.random.fold_in(key, 11)
    key_values = jax.random.fold_in(key, 12)
    levels = jnp.exp(jax.random.uniform(key_levels, (NF,), jnp.float32, math.log(0.3), math.log(3.0)))
    values = jnp.clip(jax.random.normal(key_values, (NB, 2, NF, BN), jnp.float32), -4.0, 4.0)
    scaled = values * levels[None, None, :, None]
    return scaled.reshape(NB, 2 * NF, BN).astype(jnp.bfloat16)


def with_ends(values, stream_key, smallest, largest):
    shape = values.shape
    spot = [jax.random.randint(jax.random.fold_in(stream_key, axis), (), 0, shape[axis]) for axis in range(len(shape))]
    values = values.at[tuple(spot)].set(smallest)
    longest = shape.index(max(shape))
    spot[longest] = (spot[longest] + 1) % shape[longest]
    return values.at[tuple(spot)].set(largest)


def steps_of(stream_key, extent, cuts, smallest, largest):
    loudness = 1.0
    for position, parts in cuts:
        steps = jax.random.uniform(jax.random.fold_in(jax.random.fold_in(stream_key, 6), position), (parts,), jnp.float32, smallest / len(cuts), largest / len(cuts))
        loudness = loudness * jnp.repeat(jnp.exp(steps), extent[position] // parts).reshape((-1,) + (1,) * (len(extent) - 1 - position))
    return loudness


def assign_block(rng, own, number, rows, amount, top, limit, skew):
    ranking = jax.random.permutation(rng, amount)
    crowded, usual = portions_of(amount, rows * top, limit, skew, True), portions_of(amount, rows * top, limit, skew, False)
    places = jnp.arange(amount)

    def named(lengths, rotation):
        used = int((lengths > 0).sum())
        fixed = max(1, used // 4)
        moved = fixed + (places - fixed + rotation * (used - fixed)) % max(1, amount - fixed)
        return jnp.zeros((amount,), jnp.int32).at[ranking[jnp.where(places < fixed, places, moved)]].set(jnp.asarray(lengths, jnp.int32))

    lengths = jnp.where(number % 4 == 0, named(crowded, number // 4), named(usual, number - number // 4 - 1))
    mixed = jax.random.permutation(jax.random.fold_in(own, 3), amount)
    donor, receiver = mixed[0:amount // 2 * 2:2], mixed[1:amount // 2 * 2:2]
    margin = jnp.minimum(lengths[donor] - 1, limit - lengths[receiver]) // 2
    margin = jnp.where((donor == ranking[0]) | (receiver == ranking[0]) | (lengths[receiver] == 0), 0, jnp.maximum(margin, 0))
    moved = jax.random.randint(jax.random.fold_in(own, 4), (amount // 2,), 0, 1 << 20) % (margin + 1)
    lengths = lengths.at[donor].add(-moved).at[receiver].add(moved)
    labels = jnp.searchsorted(jnp.cumsum(lengths), jnp.arange(rows * top), side="right").astype(jnp.int32)
    listing = labels.reshape(top, rows).T
    listing = listing[jax.random.permutation(jax.random.fold_in(own, 1), rows)]
    rotation = jax.random.randint(jax.random.fold_in(own, 2), (rows, 1), 0, top)
    return jnp.take_along_axis(listing, (jnp.arange(top)[None, :] + rotation) % top, axis=1)


def portions_of(number_of, total, bound, skew, full):
    loads = [(1 << 20) // math.isqrt(standing ** skew) + 1 for standing in range(1, number_of + 1)]
    largest = bound if full else min(bound, max(-(-total // number_of), total * loads[0] // sum(loads)))
    least = 1 if total - largest >= number_of - 1 else 0
    holding, surplus = [largest] + [least] * (number_of - 1), total - largest - least * (number_of - 1)
    while surplus > 0:
        movable = [i for i in range(1, number_of) if holding[i] < largest] or [i for i in range(1, number_of) if holding[i] < bound]
        whole, left = sum([loads[i] for i in movable]), surplus
        for i in movable:
            addition = min(bound - holding[i], max(1, left * loads[i] // whole), surplus)
            holding[i] = holding[i] + addition
            surplus = surplus - addition
    return np.array(holding)


def gaussian(key, extent, deviation, most, split=(), held_as=jnp.bfloat16):
    gain = steps_of(key, extent, split, -0.22, 0.18) if split else 1.0
    result = jax.random.normal(key, extent, jnp.float32) * deviation * gain
    return jnp.minimum(jnp.maximum(result, -most), most).astype(held_as)


def setup_inputs(seed: int = 0) -> dict:
    seeds = jax.random.split(jax.random.key(seed), 9)
    panels = draw_panels(jax.random.fold_in(seeds[8], 71), 0)
    tiles = gaussian(seeds[1], (NT, BN, 2 * BN), (2 * BN * TPD // NBD) ** -0.5, 0.109375, ((0, 128),))
    tile_dst = with_ends(jax.random.randint(seeds[2], (NT,), 0, NBD), jax.random.fold_in(seeds[2], 1), 0, NBD - 1).astype(jnp.int32)
    tile_src = with_ends(jax.random.randint(seeds[3], (NT,), 0, N_ROW * NBD), jax.random.fold_in(seeds[3], 1), 0, (N_ROW * NBD) - 1).astype(jnp.int32)
    geometry = gaussian(seeds[4], (NB, 6, BN), 1.0, 5.0, ((0, 128),), jnp.float32)
    areas = jnp.clip(jnp.exp(math.log(2.0) - 2.0794415 * jax.random.uniform(seeds[5], (NB, BN), jnp.float32) ** steps_of(seeds[5], (NB, BN), ((0, 128),), -0.2, 0.2)), 0.25, 2.0)
    block_owner_keys = jax.random.split(jax.random.fold_in(seeds[6], 1), NB // NBD)
    block_owner_turns = jax.random.permutation(jax.random.fold_in(seeds[6], 3), NB // NBD)
    block_owner = jax.vmap(lambda own, number: assign_block(jax.random.fold_in(seeds[6], 2), own, number, NBD, N_COL, 1, CAP, 2))(block_owner_keys, block_owner_turns).reshape((NB, 1))
    block_slot = with_ends(jax.random.randint(seeds[7], (NB,), 0, PD), jax.random.fold_in(seeds[7], 1), 0, PD - 1).astype(jnp.int32)
    return dict(panels=panels, tiles=tiles, tile_dst=tile_dst, tile_src=tile_src, geometry=geometry, areas=areas, block_owner=block_owner, block_slot=block_slot)


EPSILON = 1e-05

def make_basis(geometry, areas):
    normal = geometry[:, 0:3]
    place = geometry[:, 3:6]
    twist = jnp.stack([place[:, 1] * normal[:, 2] - place[:, 2] * normal[:, 1], place[:, 2] * normal[:, 0] - place[:, 0] * normal[:, 2], place[:, 0] * normal[:, 1] - place[:, 1] * normal[:, 0]], axis=1)
    weight = areas[:, None, :]
    return jnp.concatenate([weight * normal, weight * twist, weight, weight], axis=1)

def split_complex(images, freq_count, node_count):
    real_part = images[:, :freq_count, :node_count] - images[:, freq_count:, node_count:]
    imag_part = images[:, :freq_count, node_count:] + images[:, freq_count:, :node_count]
    return jnp.concatenate([real_part, imag_part], axis=1)

def energies(incident, field):
    freq_count = field.shape[1] // 2
    power = field[:, :freq_count] ** 2 + field[:, freq_count:] ** 2
    cross_power = incident[:, :freq_count] * field[:, :freq_count] + incident[:, freq_count:] * field[:, freq_count:]
    return (power, cross_power)

def block_moments(basis, power, cross_power):
    precise = lax.Precision.HIGHEST
    first_moments = jnp.einsum('bkn,bfn->bkf', basis[:, :7], power, precision=precise)
    last_moment = jnp.einsum('bn,bfn->bf', basis[:, 7], cross_power, precision=precise)
    joined = jnp.concatenate([first_moments, last_moment[:, None, :]], axis=1)
    return joined.reshape(joined.shape[0], -1)

def normalize(totals):
    return totals * lax.rsqrt(lax.optimization_barrier(jnp.mean(totals * totals, axis=1, keepdims=True)) + EPSILON)

def gradient_of(basis, power, cross_power, adjoint):
    precise = lax.Precision.HIGHEST
    freq_count = power.shape[1]
    shaped = adjoint.reshape(adjoint.shape[0], 8, freq_count)
    first_terms = jnp.einsum('bkf,bfn->bkn', shaped[:, :7], power, precision=precise)
    last_term = jnp.einsum('bf,bfn->bn', shaped[:, 7], cross_power, precision=precise)
    return (lax.optimization_barrier(jnp.sum(basis[:, :7] * first_terms, axis=1)) + basis[:, 7] * last_term) / freq_count

def reference(panels, tiles, tile_dst, tile_src, geometry, areas, block_owner, block_slot):
    precise = lax.Precision.HIGHEST
    block_total = panels.shape[0]
    rows_twice = panels.shape[1]
    freq_count = rows_twice // 2
    node_count = panels.shape[2]
    device_total = block_total // NBD
    tile_groups = tiles.reshape(device_total, TPD, node_count, 2 * node_count)
    dst_groups = tile_dst.reshape(device_total, TPD)
    src_groups = tile_src.reshape(device_total, TPD)

    def one_device(packed):
        device, device_tiles, device_dst, device_src = packed
        column = device % N_COL
        source = (device_src // NBD * N_COL + column) * NBD + device_src % NBD
        chosen = panels[source].astype(jnp.float32)
        images = jnp.einsum('tjn,tnm->tjm', chosen, device_tiles.astype(jnp.float32), precision=precise)
        terms = split_complex(images, freq_count, node_count)
        target = (device_dst[None, :] == jnp.arange(NBD, dtype=jnp.int32)[:, None]).astype(jnp.float32)
        return jnp.einsum('dt,tjn->djn', target, terms, precision=precise)
    near = lax.map(one_device, (jnp.arange(device_total, dtype=jnp.int32), tile_groups, dst_groups, src_groups))
    incident = panels.astype(jnp.float32)
    field = 0.5 * incident + near.reshape(block_total, rows_twice, node_count)
    power, cross_power = energies(incident, field)
    basis = make_basis(geometry, areas)
    moments = block_moments(basis, power, cross_power)
    block_index = jnp.arange(block_total, dtype=jnp.int32)
    row_index = block_index // NBD // N_COL
    particle = (row_index * N_COL + block_owner[:, 0]) * PD + block_slot
    totals = jax.ops.segment_sum(moments, particle, num_segments=PD * device_total)
    adjoint = normalize(totals)[particle]
    shape_gradient = gradient_of(basis, power, cross_power, adjoint)
    return (field, shape_gradient)
```

```python
import functools

import jax
import jax.numpy as jnp
from jax import lax
from jax.experimental import pallas as pl
from jax.experimental.pallas import tpu as pltpu
from jax.sharding import PartitionSpec as P

MESH = pl.DeviceIdType.MESH
EPSILON = 1e-05
NBD = 8
TPD = 48
NF = 16
BN = 256
PD = 4
CYCLE = 128
GROUP = 8
CHUNK = 8
H = 4
MID0 = 2
MID1 = 6

UP, DOWN, SIDE = "up", "down", "side"
MOVES = (
    (UP, 0, 0, H, NBD, None),
    (DOWN, 0, 0, H, NBD, None),
    (SIDE, 0, 0, 0, H, None),
    (UP, 0, 0, 0, H, None),
    (DOWN, 0, 0, 0, H, None),
    (SIDE, 0, 0, H, NBD, None),
    (UP, -1, 0, H, MID1, 0),
    (DOWN, 1, 0, MID1, NBD, 1),
    (UP, 0, 1, 0, H, 2),
    (DOWN, 0, 1, 0, H, 2),
    (SIDE, -1, 0, H, NBD, 0),
    (SIDE, 1, 0, H, NBD, 1),
    (UP, -1, 0, 0, MID0, 3),
    (DOWN, 1, 0, MID0, H, 4),
    (SIDE, -2, 0, H, MID1, 6),
    (SIDE, 2, 0, MID1, NBD, 7),
    (UP, -1, 1, 0, MID0, 8),
    (DOWN, 1, 1, MID0, H, 9),
)
ORDER = tuple(range(len(MOVES)))


def split2(value):
    high = value.astype(jnp.bfloat16)
    low = (value - high.astype(jnp.float32)).astype(jnp.bfloat16)
    return high, low


def nt(left, right):
    return lax.dot_general(
        left, right, (((1,), (1,)), ((), ())), preferred_element_type=jnp.float32
    )


def kernel(
    panels,
    tiles,
    tile_dst,
    tile_src,
    geometry,
    areas,
    owner,
    slot,
    field_out,
    grad_out,
    gathered,
    tile_buf,
    left_re,
    left_im,
    acc,
    geo_buf,
    area_buf,
    field_buf,
    grad_buf,
    energy_high,
    energy_low,
    key_send,
    key_all,
    moment_send,
    moment_all,
    dst_smem,
    src_smem,
    owner_smem,
    slot_smem,
    load_sem,
    tile_sem,
    out_sem,
    send_sem,
    recv_sem,
    pair_send,
    pair_recv,
    key_send_sem,
    key_recv_sem,
    mom_send_sem,
    mom_recv_sem,
    wave_sem,
):
    row = lax.axis_index("row")
    col = lax.axis_index("col")
    z = row // 4
    y = lax.rem(row // 2, 2)
    core = lax.rem(row, 2)
    y_hi = col // 4
    x = lax.rem(col, 4)

    def row_of(dz, flip, other_core=0):
        zz = lax.rem(z + dz + 4, 4)
        yy = 1 - y if flip else y
        cc = 1 - core if other_core else core
        return zz * 4 + yy * 2 + cc

    up, down, side, pair = row_of(1, 0), row_of(-1, 0), row_of(0, 1), row_of(0, 0, 1)
    target = {UP: up, DOWN: down, SIDE: side}
    near = (
        {"row": row, "col": y_hi * 4 + lax.rem(x + 1, 4)},
        {"row": row, "col": y_hi * 4 + lax.rem(x + 3, 4)},
        {"row": side, "col": col},
        {"row": side, "col": (1 - y_hi) * 4 + x},
    )
    around = near + (
        {"row": up, "col": col},
        {"row": down, "col": col},
        {"row": pair, "col": col},
    )

    barrier = pltpu.get_barrier_semaphore()
    for device in around:
        pl.semaphore_signal(barrier, inc=1, device_id=device, device_id_type=MESH)

    loads = [
        pltpu.make_async_copy(
            panels, gathered.at[pl.ds(row * NBD, NBD)], load_sem.at[0]
        ),
        pltpu.make_async_copy(owner, owner_smem, load_sem.at[1]),
        pltpu.make_async_copy(slot, slot_smem, load_sem.at[2]),
        pltpu.make_async_copy(tile_dst, dst_smem, load_sem.at[3]),
        pltpu.make_async_copy(tile_src, src_smem, load_sem.at[4]),
        pltpu.make_async_copy(geometry, geo_buf, load_sem.at[5]),
        pltpu.make_async_copy(areas, area_buf, load_sem.at[6]),
    ]
    for load in loads:
        load.start()

    def region(dz, flip, first, end, other_core=0):
        return gathered.at[pl.ds(row_of(dz, flip, other_core) * NBD + first, end - first)]

    def move_copy(number):
        way, dz, flip, first, end, _ = MOVES[number]
        if dz == 0 and flip == 0:
            source = panels.at[pl.ds(first, end - first)]
        else:
            source = region(dz, flip, first, end)
        return pltpu.make_async_remote_copy(
            src_ref=source,
            dst_ref=region(dz, flip, first, end),
            send_sem=send_sem.at[number],
            recv_sem=recv_sem.at[number],
            device_id={"row": target[way]},
            device_id_type=MESH,
        )

    def landed(number):
        way, dz, flip, first, end, _ = MOVES[number]
        if way == UP:
            return dz - 1, flip, first, end
        if way == DOWN:
            return dz + 1, flip, first, end
        return dz, 1 - flip, first, end

    def pair_copy(number):
        if number < 0:
            source, where, slot_number = panels, (0, 0, 0, NBD), len(MOVES)
            destination = region(*where)
        else:
            source = destination = region(*landed(number))
            slot_number = number
        return pltpu.make_async_remote_copy(
            src_ref=source,
            dst_ref=destination,
            send_sem=pair_send.at[slot_number],
            recv_sem=pair_recv.at[slot_number],
            device_id={"row": pair},
            device_id_type=MESH,
        )

    tile_loads = [
        pltpu.make_async_copy(
            tiles.at[pl.ds(step * CHUNK, CHUNK)],
            tile_buf.at[pl.ds(step * CHUNK, CHUNK)],
            tile_sem.at[step],
        )
        for step in range(TPD // CHUNK)
    ]

    pl.semaphore_wait(barrier, len(around))

    for number, move in enumerate(MOVES):
        if move[5] is None:
            move_copy(number).start()
    pair_copy(-1).start()
    for load in tile_loads:
        load.start()

    def wave_signal(number):
        for device in near:
            pl.semaphore_signal(
                wave_sem.at[number], inc=1, device_id=device, device_id_type=MESH
            )

    wave_signal(0)

    def arrive(number):
        move_copy(number).wait_recv()
        for later, move in enumerate(MOVES):
            if move[5] == number:
                move_copy(later).start()
        pair_copy(number).start()

    lane = lax.broadcasted_iota(jnp.int32, (1, 128), 1)
    lane_block = lane // NF

    def key_copy(step):
        return pltpu.make_async_remote_copy(
            src_ref=key_send,
            dst_ref=key_all.at[pl.ds(step * 8, 8)],
            send_sem=key_send_sem.at[step],
            recv_sem=key_recv_sem.at[step],
            device_id={"col": lax.rem(col + step, GROUP)},
            device_id_type=MESH,
        )

    def moment_copy(step):
        return pltpu.make_async_remote_copy(
            src_ref=moment_send,
            dst_ref=moment_all.at[pl.ds(step * 8, 8)],
            send_sem=mom_send_sem.at[step],
            recv_sem=mom_recv_sem.at[step],
            device_id={"col": lax.rem(col + step, GROUP)},
            device_id_type=MESH,
        )

    loads[1].wait()
    loads[2].wait()
    keys = [owner_smem[b] * PD + slot_smem[b] for b in range(NBD)]
    key_lane = jnp.zeros((8, 128), jnp.int32)
    for b in range(NBD):
        key_lane = jnp.where(lane_block == b, keys[b], key_lane)
    key_send[...] = key_lane
    key_all[pl.ds(0, 8), :] = key_lane

    wave_at = {2: 0, 5: 1, 8: 2}
    for place, number in enumerate(ORDER):
        arrive(number)
        if place in wave_at:
            wave = wave_at[place]
            pl.semaphore_wait(wave_sem.at[wave], len(near))
            if wave < 2:
                wave_signal(wave + 1)
            else:
                for step in range(1, GROUP):
                    key_copy(step).start()

    loads[5].wait()
    loads[6].wait()
    weight = area_buf[...]
    n0, n1, n2 = geo_buf[0], geo_buf[1], geo_buf[2]
    p0, p1, p2 = geo_buf[3], geo_buf[4], geo_buf[5]
    basis = jnp.concatenate(
        [
            weight * n0,
            weight * n1,
            weight * n2,
            weight * (p1 * n2 - p2 * n1),
            weight * (p2 * n0 - p0 * n2),
            weight * (p0 * n1 - p1 * n0),
            weight,
            weight,
        ],
        axis=0,
    )
    basis_high, basis_low = split2(basis)

    for load in loads[3:5]:
        load.wait()
    loads[0].wait()
    for load in tile_loads:
        load.wait()
    acc[...] = jnp.zeros_like(acc)
    pair_copy(-1).wait_recv()
    for number in ORDER:
        pair_copy(number).wait_recv()

    def step_body(step, carry):
        for inner in range(CHUNK):
            number = step * CHUNK + inner
            panel = gathered[src_smem[number]]
            turned = jnp.concatenate([-panel[NF:], panel[:NF]], axis=0)
            place = dst_smem[number]
            for d in range(NBD):
                keep = jnp.where(place == d, 1.0, 0.0).astype(jnp.float32)
                keep = jnp.full((2 * NF, BN), keep, jnp.float32).astype(jnp.bfloat16)
                rows = pl.ds(d * 2 * NF, 2 * NF)
                columns = pl.ds(inner * BN, BN)
                left_re[rows, columns] = panel * keep
                left_im[rows, columns] = turned * keep
        block = tile_buf[pl.ds(step * CHUNK, CHUNK)]
        real = block[:, :, :BN].reshape(CHUNK * BN, BN)
        imag = block[:, :, BN:].reshape(CHUNK * BN, BN)
        acc[...] += jnp.dot(
            left_re[...], real, preferred_element_type=jnp.float32
        ) + jnp.dot(left_im[...], imag, preferred_element_type=jnp.float32)
        return carry

    lax.fori_loop(0, TPD // CHUNK, step_body, 0)

    for b in range(NBD):
        incident = gathered[row * NBD + b].astype(jnp.float32)
        field = 0.5 * incident + acc[pl.ds(b * 2 * NF, 2 * NF), :]
        field_buf[b] = field
        re, im = field[:NF], field[NF:]
        high, low = split2(re * re + im * im)
        energy_high[pl.ds(b * NF, NF), :] = high
        energy_low[pl.ds(b * NF, NF), :] = low
        high, low = split2(incident[:NF] * re + incident[NF:] * im)
        energy_high[pl.ds(128 + b * NF, NF), :] = high
        energy_low[pl.ds(128 + b * NF, NF), :] = low

    field_copy = pltpu.make_async_copy(field_buf, field_out, out_sem.at[0])
    field_copy.start()

    high = energy_high[...]
    low = energy_low[...]
    products = nt(basis_high, high) + nt(basis_high, low) + nt(basis_low, high)
    own = lax.broadcasted_iota(jnp.int32, (8, 128), 0) == lane_block
    row_index = lax.broadcasted_iota(jnp.int32, (8, 128), 0)
    moments = jnp.zeros((8, 128), jnp.float32)
    for k in range(8):
        side_columns = slice(0, 128) if k < 7 else slice(128, 256)
        part = jnp.where(own, products[k * 8 : k * 8 + 8, side_columns], 0.0)
        total = jnp.sum(part, axis=0, keepdims=True)
        moments = jnp.where(row_index == k, total, moments)
    moment_send[...] = moments
    moment_all[pl.ds(0, 8), :] = moments
    for step in range(1, GROUP):
        moment_copy(step).start()

    for step in range(1, GROUP):
        key_copy(step).wait_recv()
    matches = []
    key_rows = [key_all[c * 8 : c * 8 + 1, :] for c in range(GROUP)]
    same_f = lax.broadcasted_iota(jnp.int32, (NF, 128), 0) == lax.rem(
        lax.broadcasted_iota(jnp.int32, (NF, 128), 1), NF
    )
    columns = []
    for c in range(GROUP):
        pieces = []
        for b in range(NBD):
            pieces.append(
                jnp.where(
                    jnp.logical_and(key_rows[c] == keys[b], same_f), 1.0, 0.0
                ).astype(jnp.bfloat16)
            )
        columns.append(jnp.concatenate(pieces, axis=0))

    totals = jnp.zeros((16, 128), jnp.float32)
    for c in range(GROUP):
        if c:
            moment_copy(c).wait_recv()
        high_part, low_part = split2(moment_all[c * 8 : c * 8 + 8, :])
        totals = totals + nt(jnp.concatenate([high_part, low_part], axis=0), columns[c])
    totals = totals[:8] + totals[8:]

    squares = jnp.zeros((8, 128), jnp.float32)
    lefts = []
    for k in range(8):
        spread = jnp.where(own, totals[k : k + 1, :], 0.0)
        squares = squares + spread * spread
        none = jnp.zeros_like(spread)
        lefts.append(jnp.concatenate([spread, none] if k < 7 else [none, spread], axis=1))
    left_high, left_low = split2(jnp.concatenate(lefts, axis=0))
    scale = lax.rsqrt(jnp.sum(squares, axis=1, keepdims=True) * (1.0 / 128) + EPSILON)
    dot = functools.partial(jnp.dot, preferred_element_type=jnp.float32)
    terms = (dot(left_high, high) + dot(left_high, low) + dot(left_low, high)) * basis
    gradient = terms[0:8]
    for k in range(1, 8):
        gradient = gradient + terms[k * 8 : k * 8 + 8]
    grad_buf[...] = gradient * (scale * (1.0 / NF))
    grad_copy = pltpu.make_async_copy(grad_buf, grad_out, out_sem.at[1])
    grad_copy.start()

    for number in range(len(MOVES)):
        move_copy(number).wait_send()
        pair_copy(number).wait_send()
    pair_copy(-1).wait_send()
    for step in range(1, GROUP):
        key_copy(step).wait_send()
        moment_copy(step).wait_send()
    field_copy.wait()
    grad_copy.wait()


def shards(panels, tiles, tile_dst, tile_src, geometry, areas, block_owner, block_slot):
    anywhere = pl.BlockSpec(memory_space=pl.ANY)
    count = len(MOVES)
    dma = pltpu.SemaphoreType.DMA
    return pl.pallas_call(
        kernel,
        out_shape=(
            jax.ShapeDtypeStruct((NBD, 2 * NF, BN), jnp.float32),
            jax.ShapeDtypeStruct((NBD, BN), jnp.float32),
        ),
        in_specs=[anywhere] * 8,
        out_specs=(anywhere, anywhere),
        scratch_shapes=[
            pltpu.VMEM((CYCLE, 2 * NF, BN), jnp.bfloat16),
            pltpu.VMEM((TPD, BN, 2 * BN), jnp.bfloat16),
            pltpu.VMEM((NBD * 2 * NF, CHUNK * BN), jnp.bfloat16),
            pltpu.VMEM((NBD * 2 * NF, CHUNK * BN), jnp.bfloat16),
            pltpu.VMEM((NBD * 2 * NF, BN), jnp.float32),
            pltpu.VMEM((6, NBD, BN), jnp.float32),
            pltpu.VMEM((NBD, BN), jnp.float32),
            pltpu.VMEM((NBD, 2 * NF, BN), jnp.float32),
            pltpu.VMEM((NBD, BN), jnp.float32),
            pltpu.VMEM((2 * NBD * NF, BN), jnp.bfloat16),
            pltpu.VMEM((2 * NBD * NF, BN), jnp.bfloat16),
            pltpu.VMEM((8, 128), jnp.int32),
            pltpu.VMEM((GROUP * 8, 128), jnp.int32),
            pltpu.VMEM((8, 128), jnp.float32),
            pltpu.VMEM((GROUP * 8, 128), jnp.float32),
            pltpu.SMEM((TPD,), jnp.int32),
            pltpu.SMEM((TPD,), jnp.int32),
            pltpu.SMEM((NBD,), jnp.int32),
            pltpu.SMEM((NBD,), jnp.int32),
            dma((7,)),
            dma((TPD // CHUNK,)),
            dma((2,)),
            dma((count,)),
            dma((count,)),
            dma((count + 1,)),
            dma((count + 1,)),
            dma((GROUP,)),
            dma((GROUP,)),
            dma((GROUP,)),
            dma((GROUP,)),
            pltpu.SemaphoreType.REGULAR((3,)),
        ],
        compiler_params=pltpu.CompilerParams(collective_id=0, has_side_effects=True),
    )(
        panels,
        tiles,
        tile_dst,
        tile_src,
        jnp.transpose(geometry, (1, 0, 2)),
        areas,
        block_owner.reshape(-1),
        block_slot,
    )


def solution(mesh):
    in_specs = (
        P(("row", "col"), None, None),
        P(("row", "col"), None, None),
        P(("row", "col")),
        P(("row", "col")),
        P(("row", "col"), None, None),
        P(("row", "col"), None),
        P(("row", "col"), None),
        P(("row", "col")),
    )
    out_specs = (P(("row", "col"), None, None), P(("row", "col"), None))
    return jax.shard_map(shards, mesh=mesh, in_specs=in_specs, out_specs=out_specs, check_vma=False)
```

```python
import functools

import jax
import jax.numpy as jnp
from jax import lax
from jax.experimental import pallas as pl
from jax.experimental.pallas import tpu as pltpu
from jax.sharding import PartitionSpec as P

MESH = pl.DeviceIdType.MESH
EPSILON = 1e-05
NBD = 8
TPD = 48
NF = 16
BN = 256
PD = 4
CYCLE = 128
GROUP = 8
CHUNK = 24
UNIT = 2
HALF = 128
ACROSS = 4
LAG = 8
UP, DOWN, SIDE = "up", "down", "side"


def plan_rounds():
    sends = {}

    def add(send, source, hops):
        sends[send] = (source, 2 * hops + (send[4] == 0))

    for half in range(2):
        for b in range(0, NBD, UNIT):
            upward = b % 4 < 2
            two = UP if upward else DOWN
            near, far = (-1, -2) if upward else (1, 2)
            if b < ACROSS:
                first = (SIDE, 0, 0, b, half)
                add(first, None, 2)
                for link in (UP, DOWN):
                    add((link, 0, 0, b, half), None, int(link == two))
                    add((link, 0, 1, b, half), first, int(link == two))
                add((two, near, 0, b, half), (two, 0, 0, b, half), 0)
                add((two, near, 1, b, half), (two, 0, 1, b, half), 0)
            else:
                add((SIDE, 0, 0, b, half), None, 0)
                add((UP, 0, 0, b, half), None, 2 if upward else 1)
                add((DOWN, 0, 0, b, half), None, 1 if upward else 2)
                add((SIDE, -1, 0, b, half), (UP, 0, 0, b, half), 0)
                add((SIDE, 1, 0, b, half), (DOWN, 0, 0, b, half), 0)
                add((two, near, 0, b, half), (two, 0, 0, b, half), 1)
                add((SIDE, far, 0, b, half), (two, near, 0, b, half), 0)
    left, sent, rounds = dict(sends), {}, []
    while left:
        now = []
        for link in (UP, DOWN, SIDE):
            ready = [
                send
                for send in left
                if send[0] == link
                and (left[send][0] is None or sent.get(left[send][0], len(rounds)) + LAG <= len(rounds))
            ]
            if ready:
                now.append(max(ready, key=lambda one: (left[one][1], left[one][0] is not None)))
        for send in now:
            sent[send] = len(rounds)
            del left[send]
        rounds.append(now)
    return rounds


ROUNDS = plan_rounds()
SENT = sum(len(sends) for sends in ROUNDS) // 2
WAVES = {LAG + 5: 0, LAG + 10: 1, LAG + 15: 2}


def split2(value):
    high = value.astype(jnp.bfloat16)
    low = (value - high.astype(jnp.float32)).astype(jnp.bfloat16)
    return high, low


def nt(left, right):
    return lax.dot_general(
        left, right, (((1,), (1,)), ((), ())), preferred_element_type=jnp.float32
    )


def kernel(
    panels,
    tiles,
    tile_dst,
    tile_src,
    geometry,
    areas,
    owner,
    slot,
    field_out,
    grad_out,
    first_half,
    second_half,
    images,
    tile_buf,
    acc,
    geo_buf,
    key_send,
    key_all,
    moment_send,
    moment_all,
    tile_smem,
    block_smem,
    load_sem,
    round_sem,
    pair_sem,
    copy_sem,
    wave_sem,
):
    row = lax.axis_index("row")
    col = lax.axis_index("col")
    z = row // 4
    y = lax.rem(row // 2, 2)
    core = lax.rem(row, 2)
    y_hi = col // 4
    x = lax.rem(col, 4)

    def row_of(dz, flip, other_core=0):
        zz = lax.rem(z + dz + 4, 4)
        yy = 1 - y if flip else y
        cc = 1 - core if other_core else core
        return zz * 4 + yy * 2 + cc

    up, down, side, pair = row_of(1, 0), row_of(-1, 0), row_of(0, 1), row_of(0, 0, 1)
    target = {UP: up, DOWN: down, SIDE: side}
    near = (
        {"row": row, "col": y_hi * 4 + lax.rem(x + 1, 4)},
        {"row": row, "col": y_hi * 4 + lax.rem(x + 3, 4)},
        {"row": side, "col": col},
        {"row": side, "col": (1 - y_hi) * 4 + x},
    )
    around = near + (
        {"row": up, "col": col},
        {"row": down, "col": col},
        {"row": pair, "col": col},
    )

    barrier = pltpu.get_barrier_semaphore()
    for device in around:
        pl.semaphore_signal(barrier, inc=1, device_id=device, device_id_type=MESH)

    halves = (first_half, second_half)
    for half in range(2):
        pltpu.make_async_copy(
            panels.at[:, :, pl.ds(half * HALF, HALF)],
            halves[half].at[pl.ds(row * NBD, NBD)],
            load_sem.at[0],
        ).start()
    for place, source in enumerate((owner, slot)):
        pltpu.make_async_copy(source, block_smem.at[place], load_sem.at[1]).start()
    for place, source in enumerate((tile_dst, tile_src)):
        pltpu.make_async_copy(source, tile_smem.at[place], load_sem.at[2]).start()
    pltpu.make_async_copy(geometry, geo_buf.at[pl.ds(0, 6)], load_sem.at[3]).start()
    pltpu.make_async_copy(areas, geo_buf.at[6], load_sem.at[3]).start()

    def take(ref, sem):
        pltpu.make_async_copy(ref, ref, sem).wait()

    def blocks(half, dz, flip, b, count):
        return halves[half].at[pl.ds(row_of(dz, flip) * NBD + b, count)]

    def send(number, link, dz, flip, b, half):
        where = blocks(half, dz, flip, b, UNIT)
        pltpu.make_async_remote_copy(
            src_ref=where,
            dst_ref=where,
            send_sem=copy_sem.at[0],
            recv_sem=round_sem.at[number],
            device_id={"row": target[link]},
            device_id_type=MESH,
        ).start()

    def share(half, where):
        pltpu.make_async_remote_copy(
            src_ref=where,
            dst_ref=where,
            send_sem=copy_sem.at[1],
            recv_sem=pair_sem.at[half],
            device_id={"row": pair},
            device_id_type=MESH,
        ).start()

    def to_peers(source, destination, send_sem, recv_sem):
        for step in range(1, GROUP):
            pltpu.make_async_remote_copy(
                src_ref=source,
                dst_ref=destination.at[pl.ds(step * 8, 8)],
                send_sem=send_sem,
                recv_sem=recv_sem,
                device_id={"col": lax.rem(col + step, GROUP)},
                device_id_type=MESH,
            ).start()

    def greet(number):
        for device in near:
            pl.semaphore_signal(
                wave_sem.at[number], inc=1, device_id=device, device_id_type=MESH
            )

    take(first_half.at[pl.ds(0, 2 * NBD)], load_sem.at[0])
    pl.semaphore_wait(barrier, len(around))

    for number in range(LAG):
        for one in ROUNDS[number]:
            send(number, *one)
    for half in range(2):
        share(half, blocks(half, 0, 0, 0, NBD))
    for step in range(4):
        part = pl.ds(step * (TPD // 4), TPD // 4)
        pltpu.make_async_copy(tiles.at[part], tile_buf.at[part], load_sem.at[4]).start()
    greet(0)

    take(block_smem, load_sem.at[1])
    lane_block = lax.broadcasted_iota(jnp.int32, (8, 128), 1) // NF
    keys = [block_smem[0, b] * PD + block_smem[1, b] for b in range(NBD)]
    key_lane = jnp.zeros((8, 128), jnp.int32)
    for b in range(NBD):
        key_lane = jnp.where(lane_block == b, keys[b], key_lane)
    key_send[...] = key_lane
    key_all[pl.ds(0, 8), :] = key_lane

    for number in range(LAG, len(ROUNDS) + LAG):
        landed = ROUNDS[number - LAG]
        take(first_half.at[pl.ds(0, UNIT * len(landed))], round_sem.at[number - LAG])
        if number < len(ROUNDS):
            for one in ROUNDS[number]:
                send(number, *one)
        for link, dz, flip, b, half in landed:
            if link == SIDE:
                share(half, blocks(half, dz, 1 - flip, b, UNIT))
            else:
                share(half, blocks(half, dz + (1 if link == DOWN else -1), flip, b, UNIT))
        if number in WAVES:
            wave = WAVES[number]
            pl.semaphore_wait(wave_sem.at[wave], len(near))
            if wave < 2:
                greet(wave + 1)
            else:
                to_peers(key_send, key_all, copy_sem.at[3], copy_sem.at[4])

    take(geo_buf, load_sem.at[3])
    weight = geo_buf[6]
    n0, n1, n2 = geo_buf[0], geo_buf[1], geo_buf[2]
    p0, p1, p2 = geo_buf[3], geo_buf[4], geo_buf[5]
    basis = jnp.concatenate(
        [
            weight * n0,
            weight * n1,
            weight * n2,
            weight * (p1 * n2 - p2 * n1),
            weight * (p2 * n0 - p0 * n2),
            weight * (p0 * n1 - p1 * n0),
            weight,
            weight,
        ],
        axis=0,
    )
    basis_high, basis_low = split2(basis)

    take(tile_smem, load_sem.at[2])
    take(tile_buf, load_sem.at[4])
    acc[...] = jnp.zeros_like(acc)
    everything = pl.ds(0, UNIT * SENT + NBD)

    dot = functools.partial(jnp.dot, preferred_element_type=jnp.float32)

    def image_of(half, number):
        panel = halves[half][tile_smem[1, number]]
        turned = jnp.concatenate([-panel[NF:], panel[:NF]], axis=0)
        nodes = pl.ds(half * HALF, HALF)
        tile = jnp.concatenate(
            [tile_buf[number, nodes, pl.ds(0, BN)], tile_buf[number, nodes, pl.ds(BN, BN)]], axis=0
        )
        return dot(jnp.concatenate([panel, turned], axis=1), tile)

    def first_step(step, carry):
        for inner in range(CHUNK):
            number = step * CHUNK + inner
            images[number] = image_of(0, number)
        return carry

    def second_step(step, carry):
        for inner in range(CHUNK):
            number = step * CHUNK + inner
            image = images[number] + image_of(1, number)
            place = tile_smem[0, number]
            for d in range(NBD):
                acc[d] += jnp.where(place == d, 1.0, 0.0) * image
        return carry

    take(first_half.at[everything], pair_sem.at[0])
    lax.fori_loop(0, TPD // CHUNK, first_step, 0)
    take(second_half.at[everything], pair_sem.at[1])
    lax.fori_loop(0, TPD // CHUNK, second_step, 0)

    energies = ([], [], [], [])
    for b in range(NBD):
        incident = jnp.concatenate([part[row * NBD + b] for part in halves], axis=1).astype(jnp.float32)
        field = 0.5 * incident + acc[b]
        field_out[b] = field
        re, im = field[:NF], field[NF:]
        for place, value in enumerate((re * re + im * im, incident[:NF] * re + incident[NF:] * im)):
            first, second = split2(value)
            energies[place].append(first)
            energies[2 + place].append(second)
    high = jnp.concatenate(energies[0] + energies[1], axis=0)
    low = jnp.concatenate(energies[2] + energies[3], axis=0)
    products = nt(basis_high, high) + nt(basis_high, low) + nt(basis_low, high)
    row_index = lax.broadcasted_iota(jnp.int32, (8, 128), 0)
    own = row_index == lane_block
    moments = jnp.zeros((8, 128), jnp.float32)
    for k in range(8):
        side_columns = slice(0, 128) if k < 7 else slice(128, 256)
        part = jnp.where(own, products[k * 8 : k * 8 + 8, side_columns], 0.0)
        total = jnp.sum(part, axis=0, keepdims=True)
        moments = jnp.where(row_index == k, total, moments)
    moment_send[...] = moments
    moment_all[pl.ds(0, 8), :] = moments
    to_peers(moment_send, moment_all, copy_sem.at[5], copy_sem.at[6])

    take(key_all.at[pl.ds(8, 56)], copy_sem.at[4])
    same_f = lax.broadcasted_iota(jnp.int32, (NF, 128), 0) == lax.rem(
        lax.broadcasted_iota(jnp.int32, (NF, 128), 1), NF
    )
    columns = []
    for c in range(GROUP):
        key_row = key_all[c * 8 : c * 8 + 1, :]
        pieces = [
            jnp.where(jnp.logical_and(key_row == keys[b], same_f), 1.0, 0.0).astype(jnp.bfloat16)
            for b in range(NBD)
        ]
        columns.append(jnp.concatenate(pieces, axis=0))
    match = jnp.concatenate(columns, axis=1)

    take(moment_all.at[pl.ds(8, 56)], copy_sem.at[6])
    everyone = jnp.concatenate([moment_all[c * 8 : c * 8 + 8, :] for c in range(GROUP)], axis=1)
    totals = nt(jnp.concatenate(split2(everyone), axis=0), match)
    totals = totals[:8] + totals[8:]

    squares = jnp.zeros((8, 128), jnp.float32)
    lefts = []
    for k in range(8):
        spread = jnp.where(own, totals[k : k + 1, :], 0.0)
        squares = squares + spread * spread
        none = jnp.zeros_like(spread)
        lefts.append(jnp.concatenate([spread, none] if k < 7 else [none, spread], axis=1))
    left_high, left_low = split2(jnp.concatenate(lefts, axis=0))
    scale = lax.rsqrt(jnp.sum(squares, axis=1, keepdims=True) * (1.0 / 128) + EPSILON)
    terms = (dot(left_high, high) + dot(left_high, low) + dot(left_low, high)) * basis
    gradient = terms[0:8]
    for k in range(1, 8):
        gradient = gradient + terms[k * 8 : k * 8 + 8]
    grad_out[...] = gradient * (scale * (1.0 / NF))

    take(first_half.at[pl.ds(0, 2 * UNIT * SENT)], copy_sem.at[0])
    take(first_half.at[pl.ds(0, 2 * (UNIT * SENT + NBD))], copy_sem.at[1])
    take(key_all.at[pl.ds(8, 56)], copy_sem.at[3])
    take(moment_all.at[pl.ds(8, 56)], copy_sem.at[5])


def store(field, gradient, field_out, grad_out, sem):
    copies = [
        pltpu.make_async_copy(field, field_out, sem.at[0]),
        pltpu.make_async_copy(gradient, grad_out, sem.at[1]),
    ]
    for copy in copies:
        copy.start()
    for copy in copies:
        copy.wait()


def shards(panels, tiles, tile_dst, tile_src, geometry, areas, block_owner, block_slot):
    anywhere = pl.BlockSpec(memory_space=pl.ANY)
    vmem = pl.BlockSpec(memory_space=pltpu.VMEM)
    dma = pltpu.SemaphoreType.DMA
    field_shape = (NBD, 2 * NF, BN)
    grad_shape = (NBD, BN)
    field, gradient = pl.pallas_call(
        kernel,
        out_shape=(pltpu.VMEM(field_shape, jnp.float32), pltpu.VMEM(grad_shape, jnp.float32)),
        in_specs=[anywhere] * 8,
        out_specs=(vmem, vmem),
        scratch_shapes=[
            pltpu.VMEM((CYCLE, 2 * NF, HALF), jnp.bfloat16),
            pltpu.VMEM((CYCLE, 2 * NF, HALF), jnp.bfloat16),
            pltpu.VMEM((TPD, 2 * NF, BN), jnp.float32),
            pltpu.VMEM((TPD, BN, 2 * BN), jnp.bfloat16),
            pltpu.VMEM((NBD, 2 * NF, BN), jnp.float32),
            pltpu.VMEM((7, NBD, BN), jnp.float32),
            pltpu.VMEM((8, 128), jnp.int32),
            pltpu.VMEM((GROUP * 8, 128), jnp.int32),
            pltpu.VMEM((8, 128), jnp.float32),
            pltpu.VMEM((GROUP * 8, 128), jnp.float32),
            pltpu.SMEM((2, TPD), jnp.int32),
            pltpu.SMEM((2, NBD), jnp.int32),
            dma((5,)),
            dma((len(ROUNDS),)),
            dma((2,)),
            dma((7,)),
            pltpu.SemaphoreType.REGULAR((3,)),
        ],
        compiler_params=pltpu.CompilerParams(collective_id=0, has_side_effects=True),
    )(
        panels,
        tiles,
        tile_dst,
        tile_src,
        jnp.transpose(geometry, (1, 0, 2)),
        areas,
        block_owner.reshape(-1),
        block_slot,
    )
    return pl.pallas_call(
        store,
        out_shape=(
            jax.ShapeDtypeStruct(field_shape, jnp.float32),
            jax.ShapeDtypeStruct(grad_shape, jnp.float32),
        ),
        in_specs=[vmem, vmem],
        out_specs=(anywhere, anywhere),
        scratch_shapes=[dma((2,))],
    )(
        pltpu.with_memory_space_constraint(field, pltpu.VMEM),
        pltpu.with_memory_space_constraint(gradient, pltpu.VMEM),
    )


def solution(mesh):
    in_specs = (
        P(("row", "col"), None, None),
        P(("row", "col"), None, None),
        P(("row", "col")),
        P(("row", "col")),
        P(("row", "col"), None, None),
        P(("row", "col"), None),
        P(("row", "col"), None),
        P(("row", "col")),
    )
    out_specs = (P(("row", "col"), None, None), P(("row", "col"), None))
    return jax.shard_map(shards, mesh=mesh, in_specs=in_specs, out_specs=out_specs, check_vma=False)
```
